32 devices in a mesh: seq: 8 (over y, x, core), head: 4 (over z).
Axes of the slice: x: 2, y: 2, z: 4, core: 2. Of those that a mesh axis runs over, the one named last changes fastest.
Arguments:
- queries: bfloat16 [8192, 32, 128], P('seq', 'head'), may hold values from -6 to 6
- key_vectors: bfloat16 [8192, 32, 128], P('seq', 'head'), may hold values from -6 to 6
- value_vectors: bfloat16 [8192, 32, 128], P('seq', 'head'), may hold values from -6 to 6
- out_grad: bfloat16 [8192, 32, 128], P(('seq', 'head')), may hold values from -6 to 6
Outputs:
- attended: bfloat16 [8192, 32, 128], P(('seq', 'head'))
- query_grad: bfloat16 [8192, 32, 128], P('seq', 'head')
- key_grad: bfloat16 [8192, 32, 128], P('seq', 'head')
- value_grad: bfloat16 [8192, 32, 128], P('seq', 'head')
The draws below stay inside these ranges and needn't reach their ends.
All inputs are finite; a program needn't handle non-finite values.
Results may differ from the reference program's by a relative error of at most 0.0058.
Values may be sent and summed in bfloat16 or wider, within the bound.
No kernel may reach another device: no remote copies, remote signals or barrier semaphores. Data moves between devices by JAX's collectives and lax.ppermute only.
A program may use at most 128 MiB of HBM per device.

```python
import jax
import jax.numpy as jnp
from jax import lax

H = 32
HD = 128
TOK_DEV = 1024
TOKENS = 8192
N_SEQ = 8


def steps_of(rng, extent, pieces, least, largest):
    def one(dim, blocks):
        draws = jax.random.uniform(jax.random.fold_in(jax.random.fold_in(rng, 6), dim), (blocks,), jnp.float32, least / len(pieces), largest / len(pieces))
        return jnp.repeat(jnp.exp(draws), extent[dim] // blocks).reshape((-1,) + (1,) * (len(extent) - dim - 1))

    gain = one(*pieces[0])
    for cut in pieces[1:]:
        gain = gain * one(*cut)
    return gain


def scatter_about(key, extent, width, bound, shards=(), kind=jnp.bfloat16):
    factor_of = steps_of(key, extent, shards, -0.22, 0.18) if shards else 1.0
    values = jax.random.normal(key, extent, jnp.float32) * width * factor_of
    return jnp.minimum(jnp.maximum(values, -bound), bound).astype(kind)


def setup_inputs(seed: int = 0) -> dict:
    splits = jax.random.split(jax.random.key(seed), 5)
    queries = scatter_about(splits[0], (TOKENS, H, HD), 1.0, 6.0, ((0, 8), (1, 4)))
    key_vectors = scatter_about(splits[1], (TOKENS, H, HD), 1.0, 6.0, ((0, 8), (1, 4)))
    value_vectors = scatter_about(splits[2], (TOKENS, H, HD), 1.0, 6.0, ((0, 8), (1, 4)))
    out_grad = scatter_about(splits[3], (TOKENS, H, HD), 1.0, 6.0, ((0, 32),))
    return {"queries": queries, "key_vectors": key_vectors, "value_vectors": value_vectors, "out_grad": out_grad}


def bf_round(values):
    return lax.optimization_barrier(values.astype(jnp.bfloat16)).astype(jnp.float32)

def seg_scaling(seg_index):
    position = (seg_index * TOK_DEV + jnp.arange(TOK_DEV, dtype=jnp.int32)).astype(jnp.float32)
    return 1.0 / jnp.sqrt(HD * (position + 1.0))

def reference(queries, key_vectors, value_vectors, out_grad):
    shape_seg = (N_SEQ, TOK_DEV, H, HD)
    query_seg = queries.reshape(shape_seg)
    key_seg = key_vectors.reshape(shape_seg)
    value_seg = value_vectors.reshape(shape_seg)
    grad_seg = out_grad.reshape(shape_seg)
    seg_ids = jnp.arange(N_SEQ, dtype=jnp.int32)

    def states(items):
        query_part, key_part, value_part, grad_part, seg_index = items
        scaling = seg_scaling(seg_index)
        scaled_grad = (scaling[:, None, None] * grad_part.astype(jnp.float32)).astype(jnp.bfloat16)
        seg_state = jnp.einsum('shd,she->hde', key_part.astype(jnp.float32), value_part.astype(jnp.float32))
        grad_state = jnp.einsum('thd,the->hde', query_part.astype(jnp.float32), scaled_grad.astype(jnp.float32))
        return (seg_state, grad_state, scaled_grad)
    seg_state, grad_state, scaled_all = lax.map(states, (query_seg, key_seg, value_seg, grad_seg, seg_ids))
    zero_state = jnp.zeros((1, H, HD, HD), jnp.float32)
    prefix_all = jnp.concatenate([zero_state, jnp.cumsum(seg_state, axis=0)[:-1]], axis=0).astype(jnp.bfloat16)
    later_incl = jnp.flip(jnp.cumsum(jnp.flip(grad_state, 0), axis=0), 0)
    suffix_all = jnp.concatenate([later_incl[1:], zero_state], axis=0).astype(jnp.bfloat16)
    causal = (jnp.arange(TOK_DEV)[None, :] <= jnp.arange(TOK_DEV)[:, None])[None]

    def outputs(items):
        query_part, key_part, value_part, scaled_grad, prefix, suffix, seg_index = items
        scaling = seg_scaling(seg_index)
        query_f = query_part.astype(jnp.float32)
        key_f = key_part.astype(jnp.float32)
        value_f = value_part.astype(jnp.float32)
        grad_f = scaled_grad.astype(jnp.float32)
        prefix_f = prefix.astype(jnp.float32)
        suffix_f = suffix.astype(jnp.float32)
        within = bf_round(jnp.where(causal, jnp.einsum('thd,shd->hts', query_f, key_f), 0.0))
        grad_scores = bf_round(jnp.where(causal, jnp.einsum('thd,shd->hts', grad_f, value_f), 0.0))
        attended = scaling[:, None, None] * (jnp.einsum('thd,hde->the', query_f, prefix_f) + jnp.einsum('hts,shd->thd', within, value_f))
        query_grad = jnp.einsum('the,hde->thd', grad_f, prefix_f) + jnp.einsum('hts,shd->thd', grad_scores, key_f)
        key_grad = jnp.einsum('shj,hij->shi', value_f, suffix_f) + jnp.einsum('hts,thd->shd', grad_scores, query_f)
        value_grad = jnp.einsum('shi,hij->shj', key_f, suffix_f) + jnp.einsum('hts,the->she', within, grad_f)
        return (attended.astype(jnp.bfloat16), query_grad.astype(jnp.bfloat16), key_grad.astype(jnp.bfloat16), value_grad.astype(jnp.bfloat16))
    attended, query_grad, key_grad, value_grad = lax.map(outputs, (query_seg, key_seg, value_seg, scaled_all, prefix_all, suffix_all, seg_ids))
    full_shape = (N_SEQ * TOK_DEV, H, HD)
    return (attended.reshape(full_shape), query_grad.reshape(full_shape), key_grad.reshape(full_shape), value_grad.reshape(full_shape))
```

```python
import jax
import jax.numpy as jnp
from jax import lax
from jax.experimental import pallas as pl
from jax.experimental.pallas import tpu as pltpu
from jax.sharding import PartitionSpec as P


F32 = jnp.float32
BF16 = jnp.bfloat16


def dot(lhs, rhs, lhs_dim, rhs_dim):
    return lax.dot_general(
        lhs, rhs, (((lhs_dim,), (rhs_dim,)), ((), ())), preferred_element_type=F32
    )


def iota(rows, dim):
    return lax.broadcasted_iota(jnp.int32, (rows, rows), dim)


def masked(mask, scores):
    return jnp.where(mask, scores, 0.0).astype(BF16)


def key_state_kernel(key_ref, value_ref, key_out, value_out, before_ref, total_ref, running):
    @pl.when(pl.program_id(0) == 0)
    def _():
        running[...] = jnp.zeros_like(running)

    key_out[...] = jnp.swapaxes(key_ref[...], 0, 1)
    value_out[...] = jnp.swapaxes(value_ref[...], 0, 1)
    before_ref[:, 0] = running[...]
    for h in range(running.shape[0]):
        running[h] += dot(key_out[h], value_out[h], 0, 0)
    total_ref[...] = running[...]


def attended_kernel(index_ref, query_ref, key_ref, value_ref, before_ref, prefix_ref, scale_ref, out_ref, held):
    block, rows = query_ref.shape[:2]
    mask = iota(rows, 1) <= iota(rows, 0)
    scale = scale_ref[...]
    first = pl.program_id(0) * block
    for h in range(block):
        query = query_ref[h]
        state = (prefix_ref[h] + before_ref[h, 0]).astype(BF16)
        within = masked(mask, dot(query, key_ref[h], 1, 1))
        total = dot(query, state, 1, 0) + dot(within, value_ref[h], 1, 0)
        held[first + h] = (scale * total).astype(BF16)

    @pl.when(pl.program_id(0) == pl.num_programs(0) - 1)
    def _():
        out_ref[...] = jnp.swapaxes(held[...], 0, 1)


def grad_state_kernel(index_ref, piece_ref, query_ref, scale_ref, grad_ref, state_ref):
    scale = scale_ref[...][:, None, :]
    scaled = (scale * piece_ref[...].astype(F32)).astype(BF16)
    grad_ref[...] = jnp.swapaxes(scaled, 0, 1)
    for h in range(grad_ref.shape[0]):
        state_ref[h] = dot(query_ref[h], grad_ref[h], 0, 0)


def local_grad_kernel(index_ref, query_ref, key_ref, value_ref, grad_ref, before_ref, prefix_ref, *refs):
    query_out, key_out, value_out, held = refs[-4:]
    block, rows = query_ref.shape[:2]
    lower = iota(rows, 1) <= iota(rows, 0)
    upper = iota(rows, 0) <= iota(rows, 1)
    first = pl.program_id(0) * block
    for h in range(block):
        query, key, value, grad = query_ref[h], key_ref[h], value_ref[h], grad_ref[h]
        state = (prefix_ref[h] + before_ref[h, 0]).astype(BF16)
        scores = masked(lower, dot(grad, value, 1, 1))
        held[first + h] = (dot(grad, state, 1, 1) + dot(scores, key, 1, 0)).astype(BF16)
        key_out[h] = dot(masked(upper, dot(value, grad, 1, 1)), query, 1, 0)
        value_out[h] = dot(masked(upper, dot(key, query, 1, 1)), grad, 1, 0)

    @pl.when(pl.program_id(0) == pl.num_programs(0) - 1)
    def _():
        query_out[...] = jnp.swapaxes(held[...], 0, 1)


def later_grad_kernel(index_ref, key_ref, value_ref, key_part, value_part, suffix_ref, *refs):
    states = refs[:-4]
    key_out, value_out, key_held, value_held = refs[-4:]
    c = pl.program_id(0)
    for h in range(key_ref.shape[0]):
        state = suffix_ref[h]
        for r, state_ref in enumerate(states):
            state = state + jnp.where(index_ref[r] > c, state_ref[h], 0.0)
        state = state.astype(BF16)
        key_held[h] = (key_part[h] + dot(value_ref[h], state, 1, 1)).astype(BF16)
        value_held[h] = (value_part[h] + dot(key_ref[h], state, 1, 0)).astype(BF16)
    key_out[...] = jnp.swapaxes(key_held[...], 0, 1)
    value_out[...] = jnp.swapaxes(value_held[...], 0, 1)


def cost(flops, size):
    return pl.CostEstimate(flops=int(flops), bytes_accessed=int(size), transcendentals=0)


def other_segments(total, later, n_seq):
    core = lax.axis_index("seq") % 2
    half = total.shape[0] // 2
    swap = [(i, i ^ 1) for i in range(n_seq)]
    twin = lax.ppermute(total, "seq", swap)
    mine = lax.dynamic_slice_in_dim(total + twin, core * half, half, 0)
    acc = jnp.zeros_like(mine)
    for step in range(n_seq // 2 - 1, 0, -1):
        hops = [(i, i + 2 * step) for i in range(n_seq - 2 * step)]
        if later:
            hops = [(b, a) for a, b in hops]
        acc = acc + lax.ppermute(mine, "seq", hops)
    theirs = lax.ppermute(acc, "seq", swap)
    low = core == 0
    both = jnp.concatenate([jnp.where(low, acc, theirs), jnp.where(low, theirs, acc)], axis=0)
    use_twin = low if later else jnp.logical_not(low)
    return both + jnp.where(use_twin, twin, 0.0)


def per_device(n_seq, n_head, queries, key_vectors, value_vectors, out_grad):
    tok_rows, heads, size = queries.shape
    chunk = out_grad.shape[0]
    n_chunk = tok_rows // chunk
    block = max(heads // 2, 1)
    me = lax.axis_index("head")
    order = sorted(range(1, n_head), reverse=True)
    array = jax.ShapeDtypeStruct
    index = {r: jnp.reshape(me ^ r, (1,)).astype(jnp.int32) for r in range(n_head)}
    chunk_of = jnp.stack([me ^ r for r in range(n_head)]).astype(jnp.int32)

    pieces = {}
    for r in order:
        piece = lax.dynamic_slice_in_dim(out_grad, (me ^ r) * heads, heads, 1)
        pieces[r] = lax.ppermute(piece, "head", [(i, i ^ r) for i in range(n_head)])
    pieces[0] = lax.dynamic_slice_in_dim(out_grad, me * heads, heads, 1)

    position = (lax.axis_index("seq") * tok_rows + lax.iota(jnp.int32, tok_rows)).astype(F32)
    scaling = 1.0 / jnp.sqrt(size * (position + 1.0))
    scale = jnp.broadcast_to(scaling[:, None], (tok_rows, size))

    full_bytes = heads * tok_rows * size * 2
    unit = 2 * heads * tok_rows * size * chunk

    by_token = pl.BlockSpec((chunk, heads, size), lambda c, *_: (c, 0, 0))
    by_head = pl.BlockSpec((heads, chunk, size), lambda c, *_: (0, c, 0))
    all_states = pl.BlockSpec((heads, size, size), lambda *_: (0, 0, 0))
    head_shape = array((heads, tok_rows, size), BF16)
    state_shape = array((heads, size, size), F32)
    key, value, before, key_total = pl.pallas_call(
        key_state_kernel,
        grid=(n_chunk,),
        in_specs=[by_token, by_token],
        out_specs=[
            by_head,
            by_head,
            pl.BlockSpec((heads, 1, size, size), lambda c: (0, c, 0, 0)),
            all_states,
        ],
        out_shape=[head_shape, head_shape, array((heads, n_chunk, size, size), F32), state_shape],
        scratch_shapes=[pltpu.VMEM((heads, size, size), F32)],
        cost_estimate=cost(unit, 5 * full_bytes),
        name="key_state",
    )(key_vectors, value_vectors)
    query = jnp.transpose(queries, (1, 0, 2))
    prefix = other_segments(key_total, False, n_seq)

    rows_spec = pl.BlockSpec((block, chunk, size), lambda h, i: (h, i[0], 0))
    before_spec = pl.BlockSpec((block, 1, size, size), lambda h, i: (h, i[0], 0, 0))
    some_states = pl.BlockSpec((block, size, size), lambda h, i: (h, 0, 0))
    scale_spec = pl.BlockSpec((chunk, size), lambda h, i: (i[0], 0))
    piece_spec = pl.BlockSpec((chunk, heads, size), lambda h, i: (0, 0, 0))

    arrived = {}
    for r in order + [0]:
        part = pl.pallas_call(
            attended_kernel,
            grid_spec=pltpu.PrefetchScalarGridSpec(
                num_scalar_prefetch=1,
                grid=(heads // block,),
                in_specs=[rows_spec] * 3 + [before_spec, some_states, scale_spec],
                out_specs=piece_spec,
                scratch_shapes=[pltpu.VMEM((heads, chunk, size), BF16)],
            ),
            out_shape=array((chunk, heads, size), BF16),
            cost_estimate=cost(3 * unit // n_chunk, 5 * full_bytes // n_chunk),
            name="attended",
        )(index[r], query, key, value, before, prefix, scale)
        arrived[r] = lax.ppermute(part, "head", [(i, i ^ r) for i in range(n_head)]) if r else part

    grads, states = {}, {}
    for r in [0] + order[::-1]:
        grads[r], states[r] = pl.pallas_call(
            grad_state_kernel,
            grid_spec=pltpu.PrefetchScalarGridSpec(
                num_scalar_prefetch=1,
                grid=(1,),
                in_specs=[
                    piece_spec,
                    pl.BlockSpec((heads, chunk, size), lambda h, i: (0, i[0], 0)),
                    scale_spec,
                ],
                out_specs=[pl.BlockSpec((heads, chunk, size), lambda h, i: (0, 0, 0)), all_states],
            ),
            out_shape=[array((heads, chunk, size), BF16), state_shape],
            cost_estimate=cost(unit // n_chunk, 4 * full_bytes // n_chunk),
            name="grad_state",
        )(index[r], pieces[r], query, scale)
    grad_total = sum(states[r] for r in range(1, n_head)) + states[0]
    suffix = other_segments(grad_total, True, n_seq)

    outs = ()
    out_shapes = [
        array((tok_rows, heads, size), BF16),
        array((heads, tok_rows, size), F32),
        array((heads, tok_rows, size), F32),
    ]
    for r in [0] + order[::-1]:
        outs = pl.pallas_call(
            local_grad_kernel,
            grid_spec=pltpu.PrefetchScalarGridSpec(
                num_scalar_prefetch=1,
                grid=(heads // block,),
                in_specs=[rows_spec] * 3
                + [pl.BlockSpec((block, chunk, size), lambda h, i: (h, 0, 0)), before_spec, some_states]
                + [pl.BlockSpec(memory_space=pl.ANY)] * len(outs),
                out_specs=[
                    pl.BlockSpec((chunk, heads, size), lambda h, i: (i[0], 0, 0)),
                    rows_spec,
                    rows_spec,
                ],
                scratch_shapes=[pltpu.VMEM((heads, chunk, size), BF16)],
            ),
            out_shape=out_shapes,
            input_output_aliases={7 + k: k for k in range(len(outs))},
            cost_estimate=cost(7 * unit // n_chunk, 9 * full_bytes // n_chunk),
            name="local_grad",
        )(index[r], query, key, value, grads[r], before, prefix, *outs)
    query_grad, key_part, value_part = outs

    key_grad, value_grad = pl.pallas_call(
        later_grad_kernel,
        grid_spec=pltpu.PrefetchScalarGridSpec(
            num_scalar_prefetch=1,
            grid=(n_chunk,),
            in_specs=[by_head] * 4 + [all_states] * (1 + n_head),
            out_specs=[by_token, by_token],
            scratch_shapes=[pltpu.VMEM((heads, chunk, size), BF16)] * 2,
        ),
        out_shape=[array((tok_rows, heads, size), BF16)] * 2,
        cost_estimate=cost(2 * unit, 8 * full_bytes),
        name="later_grad",
    )(chunk_of, key, value, key_part, value_part, suffix, *[states[r] for r in range(n_head)])

    attended = jnp.zeros((chunk, heads * n_head, size), BF16)
    for r in [0] + order:
        attended = lax.dynamic_update_slice_in_dim(attended, arrived[r], (me ^ r) * heads, 1)
    return attended, query_grad, key_grad, value_grad


def solution(mesh):
    n_seq, n_head = mesh.shape["seq"], mesh.shape["head"]

    def body(*args):
        return per_device(n_seq, n_head, *args)

    return jax.shard_map(
        body,
        mesh=mesh,
        in_specs=(
            P("seq", "head", None),
            P("seq", "head", None),
            P("seq", "head", None),
            P(("seq", "head"), None, None),
        ),
        out_specs=(
            P(("seq", "head"), None, None),
            P("seq", "head", None),
            P("seq", "head", None),
            P("seq", "head", None),
        ),
        check_vma=False,
    )
```

```python
import jax
import jax.numpy as jnp
from jax import lax
from jax.experimental import pallas as pl
from jax.experimental.pallas import tpu as pltpu
from jax.sharding import PartitionSpec as P


F32 = jnp.float32
BF16 = jnp.bfloat16
VMEM_LIMIT = 20 * 1024 * 1024
IN_VMEM = ('place', 'pick', 'local_grad', 'later_grad', 'grad_state', 'grad_state_own', 'attended')


def dot(lhs, rhs, lhs_dim, rhs_dim):
    return lax.dot_general(
        lhs, rhs, (((lhs_dim,), (rhs_dim,)), ((), ())), preferred_element_type=F32
    )


def iota(rows, dim):
    return lax.broadcasted_iota(jnp.int32, (rows, rows), dim)


def masked(mask, scores):
    return jnp.where(mask, scores, 0.0).astype(BF16)


def key_state_kernel(key_ref, value_ref, key_out, value_out, before_ref, total_ref, running):
    @pl.when(pl.program_id(0) == 0)
    def _():
        running[...] = jnp.zeros_like(running)

    key_out[...] = jnp.swapaxes(key_ref[...], 0, 1)
    value_out[...] = jnp.swapaxes(value_ref[...], 0, 1)
    before_ref[:, 0] = running[...]
    for h in range(running.shape[0]):
        running[h] += dot(key_out[h], value_out[h], 0, 0)
    total_ref[...] = running[...]


def base_state(held_refs, core, j, later, half, h):
    twin_ref, mine_ref, theirs_ref = held_refs
    use_twin = core == (0 if later else 1)
    own = jnp.where(core == j, mine_ref[h], theirs_ref[h])
    return own + jnp.where(use_twin, twin_ref[j * half + h], 0.0)


def attended_kernel(n_head, index_ref, query_ref, key_ref, value_ref, before_ref, scale_ref, *refs):
    prefix_refs, outs, held, base = refs[:3], refs[3:-2], refs[-2], refs[-1]
    r, j = pl.program_id(0), pl.program_id(1)
    half, rows = query_ref.shape[:2]
    mask = iota(rows, 1) <= iota(rows, 0)
    scale = scale_ref[...]

    @pl.when(r == 0)
    def _():
        for h in range(half):
            base[j * half + h] = base_state(prefix_refs, index_ref[1], j, False, half, h)

    for h in range(half):
        query = query_ref[h]
        state = (base[j * half + h] + before_ref[h, 0]).astype(BF16)
        within = masked(mask, dot(query, key_ref[h], 1, 1))
        total = dot(query, state, 1, 0) + dot(within, value_ref[h], 1, 0)
        held[j * half + h] = (scale * total).astype(BF16)
    for step in range(n_head):

        @pl.when((j == 1) & (r == step))
        def _():
            outs[step - 1][...] = jnp.swapaxes(held[...], 0, 1)


def grad_state_kernel(n_piece, index_ref, query_ref, scale_ref, *refs):
    pieces = refs[:n_piece]
    grad_ref, state_ref, total_ref = refs[-3:]
    step = pl.program_id(0)
    scale = scale_ref[...][:, None, :]
    for k, piece_ref in enumerate(pieces):

        @pl.when(step == k)
        def _():
            scaled = (scale * piece_ref[...].astype(F32)).astype(BF16)
            grad_ref[...] = jnp.swapaxes(scaled, 0, 1)

    @pl.when(step == 0)
    def _():
        total_ref[...] = refs[n_piece][...] if len(refs) > n_piece + 3 else jnp.zeros_like(total_ref)

    for h in range(grad_ref.shape[0]):
        state = dot(query_ref[h], grad_ref[h], 0, 0)
        state_ref[0, h] = state
        total_ref[h] += state


def local_grad_kernel(index_ref, query_ref, key_ref, value_ref, grad_ref, before_ref, *refs):
    prefix_refs = refs[:3]
    query_out, key_out, value_out, held, base = refs[3:]
    j = pl.program_id(1)
    half, rows = query_ref.shape[:2]
    lower = iota(rows, 1) <= iota(rows, 0)
    upper = iota(rows, 0) <= iota(rows, 1)

    @pl.when(pl.program_id(0) == 0)
    def _():
        for h in range(half):
            base[j * half + h] = base_state(prefix_refs, index_ref[1], j, False, half, h)

    for h in range(half):
        query, key, value, grad = query_ref[h], key_ref[h], value_ref[h], grad_ref[h]
        state = (base[j * half + h] + before_ref[h, 0]).astype(BF16)
        scores = masked(lower, dot(grad, value, 1, 1))
        held[j * half + h] = (dot(grad, state, 1, 1) + dot(scores, key, 1, 0)).astype(BF16)
        key_out[h] = dot(masked(upper, dot(value, grad, 1, 1)), query, 1, 0)
        value_out[h] = dot(masked(upper, dot(key, query, 1, 1)), grad, 1, 0)

    @pl.when(j == 1)
    def _():
        query_out[...] = jnp.swapaxes(held[...], 0, 1)


def later_grad_kernel(index_ref, key_ref, value_ref, key_part, value_part, state_ref, *refs):
    suffix_refs = refs[:3]
    key_out, value_out, running, key_held, value_held = refs[3:]
    half = running.shape[0] // 2

    @pl.when(pl.program_id(0) == 0)
    def _():
        for h in range(2 * half):
            running[h] = base_state(suffix_refs, index_ref[1], h // half, True, half, h % half)

    for h in range(2 * half):
        state = running[h].astype(BF16)
        running[h] += state_ref[0, h]
        key_held[h] = (key_part[h] + dot(value_ref[h], state, 1, 1)).astype(BF16)
        value_held[h] = (value_part[h] + dot(key_ref[h], state, 1, 0)).astype(BF16)
    key_out[...] = jnp.swapaxes(key_held[...], 0, 1)
    value_out[...] = jnp.swapaxes(value_held[...], 0, 1)


def pick_kernel(steps, heads, index_ref, source_ref, *refs):
    outs, sem = refs[:-1], refs[-1]
    copies = []
    for k, step in enumerate(steps):
        at = pl.ds(pl.multiple_of((index_ref[0] ^ step) * heads, heads), heads)
        copies.append(pltpu.make_async_copy(source_ref.at[:, at], outs[k], sem.at[k]))
    for copy in copies:
        copy.start()
    for copy in copies:
        copy.wait()


def place_kernel(steps, heads, index_ref, *refs):
    pieces, out_ref, sem = refs[: len(steps)], refs[-2], refs[-1]
    copies = []
    for k, step in enumerate(steps):
        at = pl.ds(pl.multiple_of((index_ref[0] ^ step) * heads, heads), heads)
        copies.append(pltpu.make_async_copy(pieces[k], out_ref.at[:, at], sem.at[k]))
    for copy in copies:
        copy.start()
    for copy in copies:
        copy.wait()


def cost(flops, size):
    return pl.CostEstimate(flops=int(flops), bytes_accessed=int(size), transcendentals=0)


def other_segments(total, later, n_seq):
    core = lax.axis_index("seq") % 2
    half = total.shape[0] // 2
    swap = [(i, i ^ 1) for i in range(n_seq)]
    twin = lax.ppermute(total, "seq", swap)
    mine = lax.dynamic_slice_in_dim(total + twin, core * half, half, 0)
    acc = jnp.zeros_like(mine)
    for step in range(n_seq // 2 - 1, 0, -1):
        hops = [(i, i + 2 * step) for i in range(n_seq - 2 * step)]
        if later:
            hops = [(b, a) for a, b in hops]
        acc = acc + lax.ppermute(mine, "seq", hops)
    theirs = lax.ppermute(acc, "seq", swap)
    return twin, acc, theirs


def per_device(n_seq, n_head, queries, key_vectors, value_vectors, out_grad):
    tok_rows, heads, size = queries.shape
    chunk = out_grad.shape[0]
    n_chunk = tok_rows // chunk
    me = lax.axis_index("head")
    order = sorted(range(1, n_head), reverse=True)
    array = jax.ShapeDtypeStruct
    core = lax.axis_index("seq") % 2
    place = jnp.stack([me, core]).astype(jnp.int32)
    any_spec = pl.BlockSpec(memory_space=pl.ANY)

    def call(kernel, grid, in_specs, out_specs, out_shape, scratch, estimate, name, aliases={}):
        small = {"vmem_limit_bytes": VMEM_LIMIT} if name in IN_VMEM else {}
        return pl.pallas_call(
            kernel,
            grid_spec=pltpu.PrefetchScalarGridSpec(
                num_scalar_prefetch=1,
                grid=grid,
                in_specs=in_specs,
                out_specs=out_specs,
                scratch_shapes=scratch,
            ),
            out_shape=out_shape,
            input_output_aliases=aliases,
            cost_estimate=estimate,
            compiler_params=pltpu.CompilerParams(**small),
        )

    whole_piece = pl.BlockSpec((chunk, heads, size), lambda *_: (0, 0, 0))
    piece_shape = array((chunk, heads, size), BF16)
    in_vmem = pl.BlockSpec(memory_space=pltpu.VMEM)
    aligned = heads % 8 == 0

    def hbm(*values):
        return [pltpu.with_memory_space_constraint(value, pltpu.HBM) for value in values]

    def pick(steps):
        if not aligned:
            return [lax.dynamic_slice_in_dim(out_grad, (me ^ r) * heads, heads, 1) for r in steps]
        return call(
            lambda *refs: pick_kernel(steps, heads, *refs),
            (1,),
            [any_spec],
            [in_vmem] * len(steps),
            [piece_shape] * len(steps),
            [pltpu.SemaphoreType.DMA((len(steps),))],
            cost(0, 4 * chunk * heads * size * len(steps)),
            "pick",
        )(place, *hbm(out_grad))

    pieces = {}
    picked = dict(zip(order[:1], pick(order[:1])))
    picked.update(zip(order[1:] + [0], pick(order[1:] + [0])))
    for r in order:
        pieces[r] = lax.ppermute(picked[r], "head", [(i, i ^ r) for i in range(n_head)])
    pieces[0] = picked[0]

    position = (lax.axis_index("seq") * tok_rows + lax.iota(jnp.int32, tok_rows)).astype(F32)
    scaling = 1.0 / jnp.sqrt(size * (position + 1.0))
    scale = jnp.broadcast_to(scaling[:, None], (tok_rows, size))

    full_bytes = heads * tok_rows * size * 2
    unit = 2 * heads * tok_rows * size * chunk
    half = heads // 2

    by_token = pl.BlockSpec((chunk, heads, size), lambda c, *_: (c, 0, 0))
    by_head = pl.BlockSpec((heads, chunk, size), lambda c, *_: (0, c, 0))
    all_states = pl.BlockSpec((heads, size, size), lambda *_: (0, 0, 0))
    head_shape = array((heads, tok_rows, size), BF16)
    state_shape = array((heads, size, size), F32)
    states_shape = array((n_chunk, heads, size, size), F32)
    key, value, before, key_total = pl.pallas_call(
        key_state_kernel,
        grid=(n_chunk,),
        in_specs=[by_token, by_token],
        out_specs=[
            by_head,
            by_head,
            pl.BlockSpec((heads, 1, size, size), lambda c: (0, c, 0, 0)),
            all_states,
        ],
        out_shape=[head_shape, head_shape, array((heads, n_chunk, size, size), F32), state_shape],
        scratch_shapes=[pltpu.VMEM((heads, size, size), F32)],
        cost_estimate=cost(unit, 5 * full_bytes),
        name="key_state",
    )(key_vectors, value_vectors)
    query = jnp.transpose(queries, (1, 0, 2))
    prefix = other_segments(key_total, False, n_seq)

    half_states = pl.BlockSpec((half, size, size), lambda *_: (0, 0, 0))
    other_specs = [all_states, half_states, half_states]

    def rows_of(r, j, i):
        return (j, i[0] ^ r, 0)

    rows_spec = pl.BlockSpec((half, chunk, size), rows_of)
    *parts, attended = call(
        lambda *refs: attended_kernel(n_head, *refs),
        (n_head, 2),
        [rows_spec] * 3
        + [
            pl.BlockSpec((half, 1, size, size), lambda r, j, i: (j, i[0] ^ r, 0, 0)),
            pl.BlockSpec((chunk, size), lambda r, j, i: (i[0] ^ r, 0)),
        ]
        + other_specs,
        [whole_piece] * (n_head - 1)
        + ([pl.BlockSpec((chunk, heads, size), lambda r, j, i: (0, i[0], 0))] if aligned else [whole_piece]),
        [piece_shape] * (n_head - 1)
        + ([array((chunk, heads * n_head, size), BF16)] if aligned else [piece_shape]),
        [pltpu.VMEM((heads, chunk, size), BF16), pltpu.VMEM((heads, size, size), F32)],
        cost(3 * unit, 5 * full_bytes),
        "attended",
    )(place, *hbm(query, key, value, before, scale), *prefix)
    arrived = {}
    for r in order:
        arrived[r] = lax.ppermute(parts[r - 1], "head", [(i, i ^ r) for i in range(n_head)])

    def grad_state(name, count, first, extra):
        def at(step, i):
            return i[0] ^ (step + first)

        return call(
            lambda *refs: grad_state_kernel(count, *refs[: 3 + count], *refs[3 + count : -3][:1], *refs[-3:]),
            (count,),
            [
                pl.BlockSpec((heads, chunk, size), lambda s, i: (0, at(s, i), 0)),
                pl.BlockSpec((chunk, size), lambda s, i: (at(s, i), 0)),
            ]
            + [whole_piece] * count
            + ([all_states, any_spec, any_spec] if extra else []),
            [
                pl.BlockSpec((heads, chunk, size), lambda s, i: (0, at(s, i), 0)),
                pl.BlockSpec((1, heads, size, size), lambda s, i: (at(s, i), 0, 0, 0)),
                all_states,
            ],
            [head_shape, states_shape, state_shape],
            [],
            cost(unit * count // n_chunk, 4 * full_bytes * count // n_chunk),
            name,
            {4 + count: 0, 5 + count: 1} if extra else {},
        )(place, *hbm(query, scale), *[pieces[first + k] for k in range(count)], *extra)

    grad, states, total = grad_state("grad_state_own", 1, 0, ())
    grad, states, total = grad_state("grad_state", n_head - 1, 1, (total, grad, states))
    suffix = other_segments(total, True, n_seq)

    chunk_rows = pl.BlockSpec((half, chunk, size), lambda c, j, i: (j, c, 0))
    query_grad, key_part, value_part = call(
        local_grad_kernel,
        (n_chunk, 2),
        [chunk_rows] * 4
        + [pl.BlockSpec((half, 1, size, size), lambda c, j, i: (j, c, 0, 0))]
        + other_specs,
        [pl.BlockSpec((chunk, heads, size), lambda c, j, i: (c, 0, 0)), chunk_rows, chunk_rows],
        [
            array((tok_rows, heads, size), BF16),
            array((heads, tok_rows, size), F32),
            array((heads, tok_rows, size), F32),
        ],
        [pltpu.VMEM((heads, chunk, size), BF16), pltpu.VMEM((heads, size, size), F32)],
        cost(7 * unit, 9 * full_bytes),
        "local_grad",
    )(place, *hbm(query, key, value, grad, before), *prefix)

    last_first = pl.BlockSpec((heads, chunk, size), lambda c, i: (0, n_chunk - 1 - c, 0))
    tokens_last_first = pl.BlockSpec((chunk, heads, size), lambda c, i: (n_chunk - 1 - c, 0, 0))
    key_grad, value_grad = call(
        later_grad_kernel,
        (n_chunk,),
        [last_first] * 4
        + [pl.BlockSpec((1, heads, size, size), lambda c, i: (n_chunk - 1 - c, 0, 0, 0))]
        + other_specs,
        [tokens_last_first] * 2,
        [array((tok_rows, heads, size), BF16)] * 2,
        [pltpu.VMEM((heads, size, size), F32)] + [pltpu.VMEM((heads, chunk, size), BF16)] * 2,
        cost(2 * unit, 8 * full_bytes),
        "later_grad",
    )(place, *hbm(key, value), key_part, value_part, *hbm(states), *suffix)

    for steps in (order[:1], order[1:]) if aligned else ():
        if steps:
            attended = call(
                lambda *refs, steps=steps: place_kernel(steps, heads, *refs),
                (1,),
                [in_vmem] * len(steps) + [any_spec],
                any_spec,
                array(attended.shape, BF16),
                [pltpu.SemaphoreType.DMA((len(steps),))],
                cost(0, 4 * chunk * heads * size * len(steps)),
                "place",
                {1 + len(steps): 0},
            )(place, *[arrived[r] for r in steps], attended)
    if not aligned:
        own, attended = attended, jnp.zeros((chunk, heads * n_head, size), BF16)
        for r in [0] + order:
            part = arrived[r] if r else own
            attended = lax.dynamic_update_slice_in_dim(attended, part, (me ^ r) * heads, 1)
    return attended, query_grad, key_grad, value_grad


def solution(mesh):
    n_seq, n_head = mesh.shape["seq"], mesh.shape["head"]

    def body(*args):
        return per_device(n_seq, n_head, *args)

    return jax.shard_map(
        body,
        mesh=mesh,
        in_specs=(
            P("seq", "head", None),
            P("seq", "head", None),
            P("seq", "head", None),
            P(("seq", "head"), None, None),
        ),
        out_specs=(
            P(("seq", "head"), None, None),
            P("seq", "head", None),
            P("seq", "head", None),
            P("seq", "head", None),
        ),
        check_vma=False,
    )
```

```python
import jax
import jax.numpy as jnp
from jax import lax
from jax.experimental import pallas as pl
from jax.experimental.pallas import tpu as pltpu
from jax.sharding import PartitionSpec as P


F32 = jnp.float32
BF16 = jnp.bfloat16
VMEM_LIMIT = 20 * 1024 * 1024
IN_VMEM = ('place', 'pick', 'local_grad_early', 'local_grad_last', 'later_grad', 'grad_state_early', 'grad_state_last', 'attended')


def dot(lhs, rhs, lhs_dim, rhs_dim):
    return lax.dot_general(
        lhs, rhs, (((lhs_dim,), (rhs_dim,)), ((), ())), preferred_element_type=F32
    )


def iota(rows, dim):
    return lax.broadcasted_iota(jnp.int32, (rows, rows), dim)


def masked(mask, scores):
    return jnp.where(mask, scores, 0.0).astype(BF16)


def key_state_kernel(key_ref, value_ref, key_out, value_out, before_ref, total_ref, running):
    @pl.when(pl.program_id(0) == 0)
    def _():
        running[...] = jnp.zeros_like(running)

    key_out[...] = jnp.swapaxes(key_ref[...], 0, 1)
    value_out[...] = jnp.swapaxes(value_ref[...], 0, 1)
    before_ref[:, 0] = running[...]
    for h in range(running.shape[0]):
        running[h] += dot(key_out[h], value_out[h], 0, 0)
    total_ref[...] = running[...]


def query_layout_kernel(index_ref, query_ref, query_out, scale_ref):
    rows, size = scale_ref.shape
    first = (index_ref[2] * pl.num_programs(0) + pl.program_id(0)) * rows
    position = (first + lax.broadcasted_iota(jnp.int32, (rows, size), 0)).astype(F32)
    scale_ref[...] = 1.0 / jnp.sqrt(size * (position + 1.0))
    query_out[...] = jnp.swapaxes(query_ref[...], 0, 1)


def base_state(held_refs, core, j, later, half, h):
    twin_ref, mine_ref, theirs_ref = held_refs
    use_twin = core == (0 if later else 1)
    own = jnp.where(core == j, mine_ref[h], theirs_ref[h])
    return own + jnp.where(use_twin, twin_ref[j * half + h], 0.0)


def attended_kernel(n_head, index_ref, query_ref, key_ref, value_ref, before_ref, scale_ref, *refs):
    prefix_refs, outs, held, base, scores = refs[:3], refs[3:-3], refs[-3], refs[-2], refs[-1]
    r = pl.program_id(0)
    heads, rows = query_ref.shape[:2]
    mask = iota(rows, 1) <= iota(rows, 0)
    scale = scale_ref[...]

    @pl.when(r == 0)
    def _():
        for h in range(heads):
            base[h] = base_state(prefix_refs, index_ref[1], h // (heads // 2), False, heads // 2, h % (heads // 2))

    for h in range(heads):
        scores[h] = masked(mask, dot(query_ref[h], key_ref[h], 1, 1))
    for h in range(heads):
        state = (base[h] + before_ref[h, 0]).astype(BF16)
        total = dot(query_ref[h], state, 1, 0) + dot(scores[h], value_ref[h], 1, 0)
        held[h] = (scale * total).astype(BF16)
    for step in range(n_head):

        @pl.when(r == step)
        def _():
            outs[step - 1][...] = jnp.swapaxes(held[...], 0, 1)


def grad_state_kernel(n_piece, index_ref, query_ref, scale_ref, *refs):
    pieces = refs[:n_piece]
    grad_ref, state_ref, total_ref = refs[-3:]
    step = pl.program_id(0)
    scale = scale_ref[...][:, None, :]
    for k, piece_ref in enumerate(pieces):

        @pl.when(step == k)
        def _():
            scaled = (scale * piece_ref[...].astype(F32)).astype(BF16)
            grad_ref[...] = jnp.swapaxes(scaled, 0, 1)

    @pl.when(step == 0)
    def _():
        total_ref[...] = refs[n_piece][...] if len(refs) > n_piece + 3 else jnp.zeros_like(total_ref)

    for h in range(grad_ref.shape[0]):
        state = dot(query_ref[h], grad_ref[h], 0, 0)
        state_ref[0, h] = state
        total_ref[h] += state


def local_grad_kernel(index_ref, query_ref, key_ref, value_ref, grad_ref, before_ref, *refs):
    prefix_refs = refs[:3]
    query_out, key_out, value_out, held, base = refs[3:]
    j = pl.program_id(1)
    half, rows = query_ref.shape[:2]
    lower = iota(rows, 1) <= iota(rows, 0)
    upper = iota(rows, 0) <= iota(rows, 1)

    @pl.when(pl.program_id(0) == 0)
    def _():
        for h in range(half):
            base[j * half + h] = base_state(prefix_refs, index_ref[1], j, False, half, h)

    for h in range(half):
        query, key, value, grad = query_ref[h], key_ref[h], value_ref[h], grad_ref[h]
        state = (base[j * half + h] + before_ref[h, 0]).astype(BF16)
        scores = masked(lower, dot(grad, value, 1, 1))
        held[j * half + h] = (dot(grad, state, 1, 1) + dot(scores, key, 1, 0)).astype(BF16)
        key_out[h] = dot(masked(upper, dot(value, grad, 1, 1)), query, 1, 0)
        value_out[h] = dot(masked(upper, dot(key, query, 1, 1)), grad, 1, 0)

    @pl.when(j == 1)
    def _():
        query_out[...] = jnp.swapaxes(held[...], 0, 1)


def later_grad_kernel(index_ref, key_ref, value_ref, key_part, value_part, state_ref, *refs):
    suffix_refs = refs[:3]
    key_out, value_out, running, key_held, value_held = refs[3:]
    half = running.shape[0] // 2

    @pl.when(pl.program_id(0) == 0)
    def _():
        for h in range(2 * half):
            running[h] = base_state(suffix_refs, index_ref[1], h // half, True, half, h % half)

    for h in range(2 * half):
        state = running[h].astype(BF16)
        running[h] += state_ref[0, h]
        key_held[h] = (key_part[h] + dot(value_ref[h], state, 1, 1)).astype(BF16)
        value_held[h] = (value_part[h] + dot(key_ref[h], state, 1, 0)).astype(BF16)
    key_out[...] = jnp.swapaxes(key_held[...], 0, 1)
    value_out[...] = jnp.swapaxes(value_held[...], 0, 1)


def pick_kernel(steps, heads, index_ref, source_ref, *refs):
    outs, sem = refs[:-1], refs[-1]
    copies = []
    for k, step in enumerate(steps):
        at = pl.ds(pl.multiple_of((index_ref[0] ^ step) * heads, heads), heads)
        copies.append(pltpu.make_async_copy(source_ref.at[:, at], outs[k], sem.at[k]))
    for copy in copies:
        copy.start()
    for copy in copies:
        copy.wait()


def place_kernel(steps, heads, index_ref, *refs):
    pieces, out_ref, sem = refs[: len(steps)], refs[-2], refs[-1]
    copies = []
    for k, step in enumerate(steps):
        at = pl.ds(pl.multiple_of((index_ref[0] ^ step) * heads, heads), heads)
        copies.append(pltpu.make_async_copy(pieces[k], out_ref.at[:, at], sem.at[k]))
    for copy in copies:
        copy.start()
    for copy in copies:
        copy.wait()


def send_order(n_head):
    return [n_head - 1, *range(1, n_head - 1)]


def cost(flops, size):
    return pl.CostEstimate(flops=int(flops), bytes_accessed=int(size), transcendentals=0)


def other_segments(total, later, n_seq):
    core = lax.axis_index("seq") % 2
    half = total.shape[0] // 2
    swap = [(i, i ^ 1) for i in range(n_seq)]
    twin = lax.ppermute(total, "seq", swap)
    mine = lax.dynamic_slice_in_dim(total + twin, core * half, half, 0)
    if not later:
        mine = mine.astype(BF16)
    acc = jnp.zeros(mine.shape, F32)
    for step in range(n_seq // 2 - 1, 0, -1):
        hops = [(i, i + 2 * step) for i in range(n_seq - 2 * step)]
        if later:
            hops = [(b, a) for a, b in hops]
        acc = acc + lax.ppermute(mine, "seq", hops).astype(F32)
    theirs = lax.ppermute(acc, "seq", swap)
    return twin, acc, theirs


def per_device(n_seq, n_head, queries, key_vectors, value_vectors, out_grad):
    tok_rows, heads, size = queries.shape
    chunk = out_grad.shape[0]
    n_chunk = tok_rows // chunk
    me = lax.axis_index("head")
    order = send_order(n_head)
    array = jax.ShapeDtypeStruct
    core = lax.axis_index("seq") % 2
    proc = [0] + order
    place = jnp.stack([me, core, lax.axis_index("seq")] + [me ^ r for r in proc]).astype(jnp.int32)
    any_spec = pl.BlockSpec(memory_space=pl.ANY)

    def call(kernel, grid, in_specs, out_specs, out_shape, scratch, estimate, name, aliases={}):
        small = {"vmem_limit_bytes": VMEM_LIMIT} if name in IN_VMEM else {}
        return pl.pallas_call(
            kernel,
            grid_spec=pltpu.PrefetchScalarGridSpec(
                num_scalar_prefetch=1,
                grid=grid,
                in_specs=in_specs,
                out_specs=out_specs,
                scratch_shapes=scratch,
            ),
            out_shape=out_shape,
            input_output_aliases=aliases,
            cost_estimate=estimate,
            compiler_params=pltpu.CompilerParams(**small),
        )

    whole_piece = pl.BlockSpec((chunk, heads, size), lambda *_: (0, 0, 0))
    piece_shape = array((chunk, heads, size), BF16)
    in_vmem = pl.BlockSpec(memory_space=pltpu.VMEM)
    aligned = heads % 8 == 0

    def hbm(*values):
        return [pltpu.with_memory_space_constraint(value, pltpu.HBM) for value in values]

    def pick(steps):
        if not aligned:
            return [lax.dynamic_slice_in_dim(out_grad, (me ^ r) * heads, heads, 1) for r in steps]
        return call(
            lambda *refs: pick_kernel(steps, heads, *refs),
            (1,),
            [any_spec],
            [in_vmem] * len(steps),
            [piece_shape] * len(steps),
            [pltpu.SemaphoreType.DMA((len(steps),))],
            cost(0, 4 * chunk * heads * size * len(steps)),
            "pick",
        )(place, *hbm(out_grad))

    pieces = {}
    picked = dict(zip(order[:1], pick(order[:1])))
    picked.update(zip(order[1:] + [0], pick(order[1:] + [0])))
    for r in order:
        pieces[r] = lax.ppermute(picked[r], "head", [(i, i ^ r) for i in range(n_head)])
    pieces[0] = picked[0]

    full_bytes = heads * tok_rows * size * 2
    unit = 2 * heads * tok_rows * size * chunk
    half = heads // 2

    by_token = pl.BlockSpec((chunk, heads, size), lambda c, *_: (c, 0, 0))
    by_head = pl.BlockSpec((heads, chunk, size), lambda c, *_: (0, c, 0))
    all_states = pl.BlockSpec((heads, size, size), lambda *_: (0, 0, 0))
    head_shape = array((heads, tok_rows, size), BF16)
    state_shape = array((heads, size, size), F32)
    states_shape = array((n_chunk, heads, size, size), F32)
    key, value, before, key_total = pl.pallas_call(
        key_state_kernel,
        grid=(n_chunk,),
        in_specs=[by_token, by_token],
        out_specs=[
            by_head,
            by_head,
            pl.BlockSpec((heads, 1, size, size), lambda c: (0, c, 0, 0)),
            all_states,
        ],
        out_shape=[head_shape, head_shape, array((heads, n_chunk, size, size), F32), state_shape],
        scratch_shapes=[pltpu.VMEM((heads, size, size), F32)],
        cost_estimate=cost(unit, 5 * full_bytes),
        name="key_state",
    )(key_vectors, value_vectors)
    query, scale = call(
        query_layout_kernel,
        (n_chunk,),
        [by_token],
        [by_head, pl.BlockSpec((chunk, size), lambda c, i: (c, 0))],
        [head_shape, array((tok_rows, size), F32)],
        [],
        cost(unit // 4, 2 * full_bytes),
        "query_layout",
    )(place, *hbm(queries))
    prefix = other_segments(key_total, False, n_seq)

    half_states = pl.BlockSpec((half, size, size), lambda *_: (0, 0, 0))
    other_specs = [all_states, half_states, half_states]

    rows_spec = pl.BlockSpec((heads, chunk, size), lambda r, i: (0, i[3 + r], 0))
    *parts, attended = call(
        lambda *refs: attended_kernel(n_head, *refs),
        (n_head,),
        [rows_spec] * 3
        + [
            pl.BlockSpec((heads, 1, size, size), lambda r, i: (0, i[3 + r], 0, 0)),
            pl.BlockSpec((chunk, size), lambda r, i: (i[3 + r], 0)),
        ]
        + other_specs,
        [whole_piece] * (n_head - 1)
        + ([pl.BlockSpec((chunk, heads, size), lambda r, i: (0, i[0], 0))] if aligned else [whole_piece]),
        [piece_shape] * (n_head - 1)
        + ([array((chunk, heads * n_head, size), BF16)] if aligned else [piece_shape]),
        [pltpu.VMEM((heads, chunk, size), BF16), pltpu.VMEM((heads, size, size), F32), pltpu.VMEM((heads, chunk, chunk), BF16)],
        cost(3 * unit, 5 * full_bytes),
        "attended",
    )(place, *hbm(query, key, value, before, scale), *prefix)
    arrived = {}
    for r in order:
        arrived[r] = lax.ppermute(parts[proc.index(r) - 1], "head", [(i, i ^ r) for i in range(n_head)])

    def grad_state(name, count, first, extra):
        def at(step, i):
            return i[3 + first + step]

        return call(
            lambda *refs: grad_state_kernel(count, *refs[: 3 + count], *refs[3 + count : -3][:1], *refs[-3:]),
            (count,),
            [
                pl.BlockSpec((heads, chunk, size), lambda s, i: (0, at(s, i), 0)),
                pl.BlockSpec((chunk, size), lambda s, i: (at(s, i), 0)),
            ]
            + [whole_piece] * count
            + ([all_states, any_spec, any_spec] if extra else []),
            [
                pl.BlockSpec((heads, chunk, size), lambda s, i: (0, at(s, i), 0)),
                pl.BlockSpec((1, heads, size, size), lambda s, i: (at(s, i), 0, 0, 0)),
                all_states,
            ],
            [pltpu.HBM(head_shape.shape, BF16), pltpu.HBM(states_shape.shape, F32), state_shape],
            [],
            cost(unit * count // n_chunk, 4 * full_bytes * count // n_chunk),
            name,
            {4 + count: 0, 5 + count: 1} if extra else {},
        )(place, *hbm(query, scale), *[pieces[r] for r in proc[first : first + count]], *extra)

    early = n_head
    grad, states, total = grad_state("grad_state_early", early, 0, ())
    early_grad = grad
    if early < n_head:
        grad, states, total = grad_state("grad_state_last", n_head - early, early, (total, grad, states))
    suffix = other_segments(total, True, n_seq)

    def local_grad(name, count, first, grad, outs):
        chunk_rows = pl.BlockSpec((half, chunk, size), lambda c, j, i: (j, i[3 + first + c], 0))
        return call(
            lambda *refs: local_grad_kernel(*refs[:9], *refs[9 + len(outs) :]),
            (count, 2),
            [chunk_rows] * 4
            + [pl.BlockSpec((half, 1, size, size), lambda c, j, i: (j, i[3 + first + c], 0, 0))]
            + other_specs
            + [any_spec] * len(outs),
            [pl.BlockSpec((chunk, heads, size), lambda c, j, i: (i[3 + first + c], 0, 0)), chunk_rows, chunk_rows],
            [
                array((tok_rows, heads, size), BF16),
                array((heads, tok_rows, size), F32),
                array((heads, tok_rows, size), F32),
            ],
            [pltpu.VMEM((heads, chunk, size), BF16), pltpu.VMEM((heads, size, size), F32)],
            cost(7 * unit * count // n_chunk, 9 * full_bytes * count // n_chunk),
            name,
            {9 + k: k for k in range(len(outs))},
        )(place, *hbm(query, key, value, grad, before), *prefix, *outs)

    outs = local_grad("local_grad_early", early, 0, early_grad, ())
    if early < n_head:
        outs = local_grad("local_grad_last", n_head - early, early, grad, outs)
    query_grad, key_part, value_part = outs

    last_first = pl.BlockSpec((heads, chunk, size), lambda c, i: (0, n_chunk - 1 - c, 0))
    tokens_last_first = pl.BlockSpec((chunk, heads, size), lambda c, i: (n_chunk - 1 - c, 0, 0))
    key_grad, value_grad = call(
        later_grad_kernel,
        (n_chunk,),
        [last_first] * 4
        + [pl.BlockSpec((1, heads, size, size), lambda c, i: (n_chunk - 1 - c, 0, 0, 0))]
        + other_specs,
        [tokens_last_first] * 2,
        [array((tok_rows, heads, size), BF16)] * 2,
        [pltpu.VMEM((heads, size, size), F32)] + [pltpu.VMEM((heads, chunk, size), BF16)] * 2,
        cost(2 * unit, 8 * full_bytes),
        "later_grad",
    )(place, *hbm(key, value), key_part, value_part, *hbm(states), *suffix)

    for steps in (order[:-1], order[-1:]) if aligned else ():
        if steps:
            attended = call(
                lambda *refs, steps=steps: place_kernel(steps, heads, *refs),
                (1,),
                [in_vmem] * len(steps) + [any_spec],
                any_spec,
                array(attended.shape, BF16),
                [pltpu.SemaphoreType.DMA((len(steps),))],
                cost(0, 4 * chunk * heads * size * len(steps)),
                "place",
                {1 + len(steps): 0},
            )(place, *[arrived[r] for r in steps], attended)
    if not aligned:
        own, attended = attended, jnp.zeros((chunk, heads * n_head, size), BF16)
        for r in [0] + order:
            part = arrived[r] if r else own
            attended = lax.dynamic_update_slice_in_dim(attended, part, (me ^ r) * heads, 1)
    return attended, query_grad, key_grad, value_grad


def solution(mesh):
    n_seq, n_head = mesh.shape["seq"], mesh.shape["head"]

    def body(*args):
        return per_device(n_seq, n_head, *args)

    return jax.shard_map(
        body,
        mesh=mesh,
        in_specs=(
            P("seq", "head", None),
            P("seq", "head", None),
            P("seq", "head", None),
            P(("seq", "head"), None, None),
        ),
        out_specs=(
            P(("seq", "head"), None, None),
            P("seq", "head", None),
            P("seq", "head", None),
            P("seq", "head", None),
        ),
        check_vma=False,
    )
```

```python
import jax
import jax.numpy as jnp
from jax import lax
from jax.experimental import pallas as pl
from jax.experimental.pallas import tpu as pltpu
from jax.sharding import PartitionSpec as P


F32 = jnp.float32
BF16 = jnp.bfloat16
VMEM_LIMIT = 20 * 1024 * 1024
IN_VMEM = ('place', 'pick', 'local_grad_early', 'local_grad_last', 'later_grad', 'grad_state_early', 'grad_state_last', 'attended')


def dot(lhs, rhs, lhs_dim, rhs_dim):
    return lax.dot_general(
        lhs, rhs, (((lhs_dim,), (rhs_dim,)), ((), ())), preferred_element_type=F32
    )


def iota(rows, dim):
    return lax.broadcasted_iota(jnp.int32, (rows, rows), dim)


def masked(mask, scores):
    return jnp.where(mask, scores, 0.0).astype(BF16)


def key_state_kernel(key_ref, value_ref, key_out, value_out, before_ref, total_ref, running):
    @pl.when(pl.program_id(0) == 0)
    def _():
        running[...] = jnp.zeros_like(running)

    key_out[...] = jnp.swapaxes(key_ref[...], 0, 1)
    value_out[...] = jnp.swapaxes(value_ref[...], 0, 1)
    before_ref[:, 0] = running[...]
    for h in range(running.shape[0]):
        running[h] += dot(key_out[h], value_out[h], 0, 0)
    total_ref[...] = running[...]


def query_layout_kernel(index_ref, query_ref, query_out, scale_ref):
    rows, size = scale_ref.shape
    first = (index_ref[2] * pl.num_programs(0) + pl.program_id(0)) * rows
    position = (first + lax.broadcasted_iota(jnp.int32, (rows, size), 0)).astype(F32)
    scale_ref[...] = 1.0 / jnp.sqrt(size * (position + 1.0))
    query_out[...] = jnp.swapaxes(query_ref[...], 0, 1)


def base_state(held_refs, core, j, later, half, h):
    twin_ref, mine_ref, theirs_ref = held_refs
    use_twin = core == (0 if later else 1)
    own = jnp.where(core == j, mine_ref[h], theirs_ref[h])
    return own + jnp.where(use_twin, twin_ref[j * half + h], 0.0)


def attended_kernel(n_head, index_ref, query_ref, key_ref, value_ref, before_ref, scale_ref, *refs):
    prefix_refs, outs, held, base, scores = refs[:3], refs[3:-3], refs[-3], refs[-2], refs[-1]
    r = pl.program_id(0)
    heads, rows = query_ref.shape[:2]
    mask = iota(rows, 1) <= iota(rows, 0)
    scale = scale_ref[...]

    @pl.when(r == 0)
    def _():
        for h in range(heads):
            base[h] = base_state(prefix_refs, index_ref[1], h // (heads // 2), False, heads // 2, h % (heads // 2))

    for h in range(heads):
        scores[h] = masked(mask, dot(query_ref[h], key_ref[h], 1, 1))
    for h in range(heads):
        state = (base[h] + before_ref[h, 0]).astype(BF16)
        total = dot(query_ref[h], state, 1, 0) + dot(scores[h], value_ref[h], 1, 0)
        held[h] = (scale * total).astype(BF16)
    for step in range(n_head):

        @pl.when(r == step)
        def _():
            outs[step - 1][...] = jnp.swapaxes(held[...], 0, 1)


def grad_state_kernel(n_piece, index_ref, query_ref, scale_ref, *refs):
    pieces = refs[:n_piece]
    grad_ref, state_ref, total_ref = refs[-3:]
    step = pl.program_id(0)
    scale = scale_ref[...][:, None, :]
    for k, piece_ref in enumerate(pieces):

        @pl.when(step == k)
        def _():
            scaled = (scale * piece_ref[...].astype(F32)).astype(BF16)
            grad_ref[...] = jnp.swapaxes(scaled, 0, 1)

    @pl.when(step == 0)
    def _():
        total_ref[...] = refs[n_piece][...] if len(refs) > n_piece + 3 else jnp.zeros_like(total_ref)

    for h in range(grad_ref.shape[0]):
        state = dot(query_ref[h], grad_ref[h], 0, 0)
        state_ref[0, h] = state
        total_ref[h] += state


def local_grad_kernel(index_ref, query_ref, key_ref, value_ref, grad_ref, before_ref, *refs):
    prefix_refs = refs[:3]
    query_out, key_out, value_out, held, base, scores, scores_t, within_t = refs[3:]
    heads, rows = query_ref.shape[:2]
    lower = iota(rows, 1) <= iota(rows, 0)
    upper = iota(rows, 0) <= iota(rows, 1)

    @pl.when(pl.program_id(0) == 0)
    def _():
        for h in range(heads):
            base[h] = base_state(prefix_refs, index_ref[1], h // (heads // 2), False, heads // 2, h % (heads // 2))

    for h in range(heads):
        scores[h] = masked(lower, dot(grad_ref[h], value_ref[h], 1, 1))
        scores_t[h] = masked(upper, dot(value_ref[h], grad_ref[h], 1, 1))
        within_t[h] = masked(upper, dot(key_ref[h], query_ref[h], 1, 1))
    for h in range(heads):
        state = (base[h] + before_ref[h, 0]).astype(BF16)
        held[h] = (dot(grad_ref[h], state, 1, 1) + dot(scores[h], key_ref[h], 1, 0)).astype(BF16)
        key_out[h] = dot(scores_t[h], query_ref[h], 1, 0)
        value_out[h] = dot(within_t[h], grad_ref[h], 1, 0)
    query_out[...] = jnp.swapaxes(held[...], 0, 1)


def later_grad_kernel(index_ref, key_ref, value_ref, key_part, value_part, state_ref, *refs):
    suffix_refs = refs[:3]
    key_out, value_out, running, key_held, value_held = refs[3:]
    half = running.shape[0] // 2

    @pl.when(pl.program_id(0) == 0)
    def _():
        for h in range(2 * half):
            running[h] = base_state(suffix_refs, index_ref[1], h // half, True, half, h % half)

    for h in range(2 * half):
        state = running[h].astype(BF16)
        running[h] += state_ref[0, h]
        key_held[h] = (key_part[h] + dot(value_ref[h], state, 1, 1)).astype(BF16)
        value_held[h] = (value_part[h] + dot(key_ref[h], state, 1, 0)).astype(BF16)
    key_out[...] = jnp.swapaxes(key_held[...], 0, 1)
    value_out[...] = jnp.swapaxes(value_held[...], 0, 1)


def pick_kernel(steps, heads, index_ref, source_ref, *refs):
    outs, sem = refs[:-1], refs[-1]
    copies = []
    for k, step in enumerate(steps):
        at = pl.ds(pl.multiple_of((index_ref[0] ^ step) * heads, heads), heads)
        copies.append(pltpu.make_async_copy(source_ref.at[:, at], outs[k], sem.at[k]))
    for copy in copies:
        copy.start()
    for copy in copies:
        copy.wait()


def place_kernel(steps, heads, index_ref, *refs):
    pieces, out_ref, sem = refs[: len(steps)], refs[-2], refs[-1]
    copies = []
    for k, step in enumerate(steps):
        at = pl.ds(pl.multiple_of((index_ref[0] ^ step) * heads, heads), heads)
        copies.append(pltpu.make_async_copy(pieces[k], out_ref.at[:, at], sem.at[k]))
    for copy in copies:
        copy.start()
    for copy in copies:
        copy.wait()


def send_order(n_head):
    return [n_head - 1, *range(1, n_head - 1)]


def cost(flops, size):
    return pl.CostEstimate(flops=int(flops), bytes_accessed=int(size), transcendentals=0)


def other_segments(total, later, n_seq):
    core = lax.axis_index("seq") % 2
    half = total.shape[0] // 2
    swap = [(i, i ^ 1) for i in range(n_seq)]
    twin = lax.ppermute(total, "seq", swap)
    mine = lax.dynamic_slice_in_dim(total + twin, core * half, half, 0)
    mine = mine.astype(BF16)
    acc = jnp.zeros(mine.shape, F32)
    for step in range(n_seq // 2 - 1, 0, -1):
        hops = [(i, i + 2 * step) for i in range(n_seq - 2 * step)]
        if later:
            hops = [(b, a) for a, b in hops]
        acc = acc + lax.ppermute(mine, "seq", hops).astype(F32)
    theirs = lax.ppermute(acc, "seq", swap)
    return twin, acc, theirs


def per_device(n_seq, n_head, queries, key_vectors, value_vectors, out_grad):
    tok_rows, heads, size = queries.shape
    chunk = out_grad.shape[0]
    n_chunk = tok_rows // chunk
    me = lax.axis_index("head")
    order = send_order(n_head)
    array = jax.ShapeDtypeStruct
    core = lax.axis_index("seq") % 2
    proc = [0] + order
    place = jnp.stack([me, core, lax.axis_index("seq")] + [me ^ r for r in proc]).astype(jnp.int32)
    any_spec = pl.BlockSpec(memory_space=pl.ANY)

    def call(kernel, grid, in_specs, out_specs, out_shape, scratch, estimate, name, aliases={}):
        small = {"vmem_limit_bytes": VMEM_LIMIT} if name in IN_VMEM else {}
        return pl.pallas_call(
            kernel,
            grid_spec=pltpu.PrefetchScalarGridSpec(
                num_scalar_prefetch=1,
                grid=grid,
                in_specs=in_specs,
                out_specs=out_specs,
                scratch_shapes=scratch,
            ),
            out_shape=out_shape,
            input_output_aliases=aliases,
            cost_estimate=estimate,
            compiler_params=pltpu.CompilerParams(**small),
        )

    whole_piece = pl.BlockSpec((chunk, heads, size), lambda *_: (0, 0, 0))
    piece_shape = array((chunk, heads, size), BF16)
    in_vmem = pl.BlockSpec(memory_space=pltpu.VMEM)
    aligned = heads % 8 == 0

    def hbm(*values):
        return [pltpu.with_memory_space_constraint(value, pltpu.HBM) for value in values]

    def pick(steps):
        if not aligned:
            return [lax.dynamic_slice_in_dim(out_grad, (me ^ r) * heads, heads, 1) for r in steps]
        return call(
            lambda *refs: pick_kernel(steps, heads, *refs),
            (1,),
            [any_spec],
            [in_vmem] * len(steps),
            [piece_shape] * len(steps),
            [pltpu.SemaphoreType.DMA((len(steps),))],
            cost(0, 4 * chunk * heads * size * len(steps)),
            "pick",
        )(place, *hbm(out_grad))

    pieces = {}
    picked = dict(zip(order[:1], pick(order[:1])))
    picked.update(zip(order[1:], pick(order[1:])))
    picked[0] = pick([0])[0]
    for r in order:
        pieces[r] = lax.ppermute(picked[r], "head", [(i, i ^ r) for i in range(n_head)])
    pieces[0] = picked[0]

    full_bytes = heads * tok_rows * size * 2
    unit = 2 * heads * tok_rows * size * chunk
    half = heads // 2

    by_token = pl.BlockSpec((chunk, heads, size), lambda c, *_: (c, 0, 0))
    by_head = pl.BlockSpec((heads, chunk, size), lambda c, *_: (0, c, 0))
    all_states = pl.BlockSpec((heads, size, size), lambda *_: (0, 0, 0))
    head_shape = array((heads, tok_rows, size), BF16)
    state_shape = array((heads, size, size), F32)
    states_shape = array((n_chunk, heads, size, size), F32)
    key, value, before, key_total = pl.pallas_call(
        key_state_kernel,
        grid=(n_chunk,),
        in_specs=[by_token, by_token],
        out_specs=[
            by_head,
            by_head,
            pl.BlockSpec((heads, 1, size, size), lambda c: (0, c, 0, 0)),
            all_states,
        ],
        out_shape=[head_shape, head_shape, array((heads, n_chunk, size, size), F32), state_shape],
        scratch_shapes=[pltpu.VMEM((heads, size, size), F32)],
        cost_estimate=cost(unit, 5 * full_bytes),
        name="key_state",
    )(key_vectors, value_vectors)
    query, scale = call(
        query_layout_kernel,
        (n_chunk,),
        [by_token],
        [by_head, pl.BlockSpec((chunk, size), lambda c, i: (c, 0))],
        [head_shape, array((tok_rows, size), F32)],
        [],
        cost(unit // 4, 2 * full_bytes),
        "query_layout",
    )(place, *hbm(queries))
    prefix = other_segments(key_total, False, n_seq)

    half_states = pl.BlockSpec((half, size, size), lambda *_: (0, 0, 0))
    other_specs = [all_states, half_states, half_states]

    rows_spec = pl.BlockSpec((heads, chunk, size), lambda r, i: (0, i[3 + r], 0))
    *parts, attended = call(
        lambda *refs: attended_kernel(n_head, *refs),
        (n_head,),
        [rows_spec] * 3
        + [
            pl.BlockSpec((heads, 1, size, size), lambda r, i: (0, i[3 + r], 0, 0)),
            pl.BlockSpec((chunk, size), lambda r, i: (i[3 + r], 0)),
        ]
        + other_specs,
        [whole_piece] * (n_head - 1)
        + ([pl.BlockSpec((chunk, heads, size), lambda r, i: (0, i[0], 0))] if aligned else [whole_piece]),
        [piece_shape] * (n_head - 1)
        + ([array((chunk, heads * n_head, size), BF16)] if aligned else [piece_shape]),
        [pltpu.VMEM((heads, chunk, size), BF16), pltpu.VMEM((heads, size, size), F32), pltpu.VMEM((heads, chunk, chunk), BF16)],
        cost(3 * unit, 5 * full_bytes),
        "attended",
    )(place, *hbm(query, key, value, before, scale), *prefix)
    arrived = {}
    for r in order:
        arrived[r] = lax.ppermute(parts[proc.index(r) - 1], "head", [(i, i ^ r) for i in range(n_head)])

    def grad_state(name, count, first, extra):
        def at(step, i):
            return i[3 + first + step]

        return call(
            lambda *refs: grad_state_kernel(count, *refs[: 3 + count], *refs[3 + count : -3][:1], *refs[-3:]),
            (count,),
            [
                pl.BlockSpec((heads, chunk, size), lambda s, i: (0, at(s, i), 0)),
                pl.BlockSpec((chunk, size), lambda s, i: (at(s, i), 0)),
            ]
            + [whole_piece] * count
            + ([all_states, any_spec, any_spec] if extra else []),
            [
                pl.BlockSpec((heads, chunk, size), lambda s, i: (0, at(s, i), 0)),
                pl.BlockSpec((1, heads, size, size), lambda s, i: (at(s, i), 0, 0, 0)),
                all_states,
            ],
            [pltpu.HBM(head_shape.shape, BF16), pltpu.HBM(states_shape.shape, F32), state_shape],
            [],
            cost(unit * count // n_chunk, 4 * full_bytes * count // n_chunk),
            name,
            {4 + count: 0, 5 + count: 1} if extra else {},
        )(place, *hbm(query, scale), *[pieces[r] for r in proc[first : first + count]], *extra)

    early = max(n_head - 1, 1)
    grad, states, total = grad_state("grad_state_early", early, 0, ())
    early_grad = grad
    if early < n_head:
        grad, states, total = grad_state("grad_state_last", n_head - early, early, (total, grad, states))
    suffix = other_segments(total, True, n_seq)

    def local_grad(name, count, first, grad, outs):
        chunk_rows = pl.BlockSpec((heads, chunk, size), lambda c, i: (0, i[3 + first + c], 0))
        return call(
            lambda *refs: local_grad_kernel(*refs[:9], *refs[9 + len(outs) :]),
            (count,),
            [chunk_rows] * 4
            + [pl.BlockSpec((heads, 1, size, size), lambda c, i: (0, i[3 + first + c], 0, 0))]
            + other_specs
            + [any_spec] * len(outs),
            [pl.BlockSpec((chunk, heads, size), lambda c, i: (i[3 + first + c], 0, 0)), chunk_rows, chunk_rows],
            [
                array((tok_rows, heads, size), BF16),
                array((heads, tok_rows, size), F32),
                array((heads, tok_rows, size), F32),
            ],
            [pltpu.VMEM((heads, chunk, size), BF16), pltpu.VMEM((heads, size, size), F32)]
            + [pltpu.VMEM((heads, chunk, chunk), BF16)] * 3,
            cost(7 * unit * count // n_chunk, 9 * full_bytes * count // n_chunk),
            name,
            {9 + k: k for k in range(len(outs))},
        )(place, *hbm(query, key, value, grad, before), *prefix, *outs)

    outs = local_grad("local_grad_early", early, 0, early_grad, ())
    if early < n_head:
        outs = local_grad("local_grad_last", n_head - early, early, grad, outs)
    query_grad, key_part, value_part = outs

    last_first = pl.BlockSpec((heads, chunk, size), lambda c, i: (0, n_chunk - 1 - c, 0))
    tokens_last_first = pl.BlockSpec((chunk, heads, size), lambda c, i: (n_chunk - 1 - c, 0, 0))
    key_grad, value_grad = call(
        later_grad_kernel,
        (n_chunk,),
        [last_first] * 4
        + [pl.BlockSpec((1, heads, size, size), lambda c, i: (n_chunk - 1 - c, 0, 0, 0))]
        + other_specs,
        [tokens_last_first] * 2,
        [array((tok_rows, heads, size), BF16)] * 2,
        [pltpu.VMEM((heads, size, size), F32)] + [pltpu.VMEM((heads, chunk, size), BF16)] * 2,
        cost(2 * unit, 8 * full_bytes),
        "later_grad",
    )(place, *hbm(key, value), key_part, value_part, *hbm(states), *suffix)

    for steps in (order[:-1], order[-1:]) if aligned else ():
        if steps:
            attended = call(
                lambda *refs, steps=steps: place_kernel(steps, heads, *refs),
                (1,),
                [in_vmem] * len(steps) + [any_spec],
                any_spec,
                array(attended.shape, BF16),
                [pltpu.SemaphoreType.DMA((len(steps),))],
                cost(0, 4 * chunk * heads * size * len(steps)),
                "place",
                {1 + len(steps): 0},
            )(place, *[arrived[r] for r in steps], attended)
    if not aligned:
        own, attended = attended, jnp.zeros((chunk, heads * n_head, size), BF16)
        for r in [0] + order:
            part = arrived[r] if r else own
            attended = lax.dynamic_update_slice_in_dim(attended, part, (me ^ r) * heads, 1)
    return attended, query_grad, key_grad, value_grad


def solution(mesh):
    n_seq, n_head = mesh.shape["seq"], mesh.shape["head"]

    def body(*args):
        return per_device(n_seq, n_head, *args)

    return jax.shard_map(
        body,
        mesh=mesh,
        in_specs=(
            P("seq", "head", None),
            P("seq", "head", None),
            P("seq", "head", None),
            P(("seq", "head"), None, None),
        ),
        out_specs=(
            P(("seq", "head"), None, None),
            P("seq", "head", None),
            P("seq", "head", None),
            P("seq", "head", None),
        ),
        check_vma=False,
    )
```
